32 devices in a mesh: seq: 8 (over z, y), mix: 4 (over x, core).
Axes of the slice: x: 2, y: 2, z: 4, core: 2. Of those that a mesh axis runs over, the one named last changes fastest.
Arguments:
- tokens: bfloat16 [8, 2048, 512], P('mix', 'seq'), may hold values from -6 to 6
- log_forget_rate: bfloat16 [8, 2048, 16], P('mix', 'seq'), may hold values from -0.7 to 0, as said below
- w_x: bfloat16 [512, 1024], P(None, 'mix'), may hold values from -0.25 to 0.25
- w_z: bfloat16 [512, 1024], P(None, 'mix'), may hold values from -0.25 to 0.25
- w_bc: bfloat16 [512, 128], replicated, may hold values from -0.25 to 0.25
- conv_x: bfloat16 [4, 1024], P(None, 'mix'), may hold values from -3 to 3
- conv_bc: bfloat16 [4, 128], replicated, may hold values from -3 to 3
- skip: bfloat16 [16], P('mix'), may hold values from 0.5 to 2
- gain: bfloat16 [1024], P('mix'), may hold values from 0.099609375 to 1.8984375
- w_out: bfloat16 [1024, 512], P('mix'), may hold values from -0.1875 to 0.1875
Outputs:
- mixed: bfloat16 [8, 2048, 512], P('mix', 'seq')
The draws below stay inside these ranges and needn't reach their ends.
Inputs may be any that keep to these rules, and one draw needn't show every extreme that they name: `log_forget_rate`: every entry is below zero.
All inputs are finite; a program needn't handle non-finite values.
Results may differ from the reference program's by a relative error of at most 0.012.
Values may be sent and summed in bfloat16 or wider, within the bound.
A program may use at most 128 MiB of HBM per device.

```python
import math
import jax
import jax.numpy as jnp
from jax import lax

D = 512
HEADS = 16
HEAD_DIM = 64
STATE = 64
CONV = 4
BLOCK = 128
TOK_DEV = 256
D_INNER = 1024
MIXES = 8
LENGTH = 2048


def draw_log_forget_rate(key, part):
    keys = jax.random.split(key, 6)
    slow_share = 0.5
    slow = jax.random.uniform(keys[0], (MIXES, 1, HEADS)) < slow_share
    fast_rate = jnp.exp(jax.random.uniform(keys[1], (MIXES, 1, HEADS), jnp.float32, math.log(1.0 / 50.0), math.log(1.0 / 20.0)))
    rate = jnp.where(slow, 0.5 / LENGTH, fast_rate)
    rough = jnp.exp(jax.random.uniform(keys[2], (MIXES, LENGTH, HEADS), jnp.float32, math.log(0.5), math.log(2.0)))
    blocks = LENGTH // TOK_DEV
    per_block = jnp.exp(jax.random.uniform(keys[3], (MIXES, blocks, 1, HEADS), jnp.float32, math.log(0.5), math.log(2.0)))
    per_block = jnp.broadcast_to(per_block, (MIXES, blocks, TOK_DEV, HEADS)).reshape(MIXES, LENGTH, HEADS)
    values = -rate * rough * per_block
    spots = jax.random.randint(keys[4], (MIXES, 2), 0, LENGTH)
    where_hit = jnp.any(jnp.arange(LENGTH)[None, :, None] == spots[:, None, :], axis=-1)
    strength = jax.random.uniform(keys[5], (MIXES, LENGTH, HEADS), jnp.float32, 0.25, 0.7)
    values = jnp.where(where_hit[:, :, None], jnp.minimum(values, -strength), values)
    return values.astype(jnp.bfloat16)


def levels(stream_key, dims, pieces, smallest, top_value):
    def one(axis_at, parts):
        heights = jax.random.uniform(jax.random.fold_in(jax.random.fold_in(stream_key, 6), axis_at), (parts,), jnp.float32, smallest / len(pieces), top_value / len(pieces))
        return jnp.repeat(jnp.exp(heights), dims[axis_at] // parts).reshape((-1,) + (1,) * (len(dims) - axis_at - 1))

    loudness = one(*pieces[0])
    for cut in pieces[1:]:
        loudness = loudness * one(*cut)
    return loudness


def centred(own_key, dims, scale, most, cuts=(), dtype=jnp.bfloat16):
    values = scale * jax.random.normal(own_key, dims, jnp.float32)
    if cuts:
        values = values * levels(own_key, dims, cuts, -0.22, 0.18)
    return jnp.clip(values, -most, most).astype(dtype)


def setup_inputs(seed: int = 0) -> dict:
    key_list = jax.random.split(jax.random.key(seed), 11)
    tokens = centred(key_list[0], (MIXES, LENGTH, D), 1.0, 6.0, ((0, 4), (1, 8)))
    log_forget_rate = draw_log_forget_rate(jax.random.fold_in(key_list[10], 71), 0)
    w_x = centred(key_list[2], (D, D_INNER), D ** -0.5, 0.25, ((1, 4),))
    w_z = centred(key_list[3], (D, D_INNER), D ** -0.5, 0.25, ((1, 4),))
    w_bc = centred(key_list[4], (D, 2 * STATE), D ** -0.5, 0.25)
    conv_x = centred(key_list[5], (CONV, D_INNER), CONV ** -0.5, 3.0, ((1, 4),))
    conv_bc = centred(key_list[6], (CONV, 2 * STATE), CONV ** -0.5, 3.0)
    skip = jnp.clip(0.5 + 1.5 * jax.random.uniform(key_list[7], (HEADS,), jnp.float32) ** levels(key_list[7], (HEADS,), ((0, 4),), -0.2, 0.2), 0.5, 2.0).astype(jnp.bfloat16)
    gain = jnp.clip(1.0 + 0.18 * jax.random.normal(key_list[8], (D_INNER,), jnp.float32), 0.099609375, 1.8984375).astype(jnp.bfloat16)
    w_out = centred(key_list[9], (D_INNER, D), D_INNER ** -0.5, 0.1875, ((0, 4),))
    return dict(tokens=tokens, log_forget_rate=log_forget_rate, w_x=w_x, w_z=w_z, w_bc=w_bc, conv_x=conv_x, conv_bc=conv_bc, skip=skip, gain=gain, w_out=w_out)


def conv_silu(pre, taps):
    length = pre.shape[0]
    padded_sequence = jnp.pad(pre.astype(jnp.float32), ((CONV - 1, 0), (0, 0)))
    total = jnp.zeros((length, pre.shape[1]), jnp.float32)
    for k in range(CONV):
        total = total + taps[k].astype(jnp.float32)[None, :] * padded_sequence[k:k + length]
    return jax.nn.silu(total).astype(jnp.bfloat16)

def reference(tokens, log_forget_rate, w_x, w_z, w_bc, conv_x, conv_bc, skip, gain, w_out):
    mask = jnp.tril(jnp.ones((BLOCK, BLOCK), bool))[:, :, None]
    skip_f = skip.astype(jnp.float32)
    gain_f = gain.astype(jnp.float32).reshape(HEADS, HEAD_DIM)

    def one_mixture(item):
        tok, decay = item
        pre_x = jnp.dot(tok, w_x, preferred_element_type=jnp.float32).astype(jnp.bfloat16)
        pre_bc = jnp.dot(tok, w_bc, preferred_element_type=jnp.float32).astype(jnp.bfloat16)
        gate_pre = jnp.dot(tok, w_z, preferred_element_type=jnp.float32).astype(jnp.bfloat16)
        x_act = conv_silu(pre_x, conv_x)
        activated_input_readout = conv_silu(pre_bc, conv_bc)
        count = LENGTH // BLOCK
        blocks = (x_act.reshape(count, BLOCK, HEADS, HEAD_DIM), activated_input_readout[:, :STATE].reshape(count, BLOCK, STATE), activated_input_readout[:, STATE:].reshape(count, BLOCK, STATE), decay.astype(jnp.float32).reshape(count, BLOCK, HEADS), gate_pre.reshape(count, BLOCK, HEADS, HEAD_DIM))

        def step(state, blk):
            xb, input_projection_rows, readout_projection_rows, ab, zb = blk
            cum = jnp.cumsum(ab, axis=0)
            scale_in = jnp.sqrt(-jnp.expm1(2.0 * ab))
            attention_scores = jnp.dot(readout_projection_rows, input_projection_rows.T, preferred_element_type=jnp.float32)
            seg = cum[:, None, :] - cum[None, :, :]
            decay_mat = jnp.where(mask, jnp.exp(jnp.where(mask, seg, -jnp.inf)), 0.0)
            weights = (decay_mat * scale_in[None, :, :] * attention_scores[:, :, None]).astype(jnp.bfloat16)
            xf = xb.astype(jnp.float32)
            intra = jnp.einsum('qkh,khp->qhp', weights.astype(jnp.float32), xf)
            inter = jnp.exp(cum)[:, :, None] * jnp.einsum('qn,hpn->qhp', readout_projection_rows.astype(jnp.float32), state, precision=lax.Precision.HIGHEST)
            tail = jnp.exp(cum[-1][None, :] - cum) * scale_in
            scaled = (xf * tail[:, :, None]).astype(jnp.bfloat16)
            block_state = jnp.einsum('khp,kn->hpn', scaled.astype(jnp.float32), input_projection_rows.astype(jnp.float32))
            new_state = jnp.exp(cum[-1])[:, None, None] * state + block_state
            y = intra + inter + skip_f[None, :, None] * xf
            v = y * jax.nn.silu(zb.astype(jnp.float32))
            normed = v * lax.rsqrt(lax.optimization_barrier(jnp.mean(v * v, axis=-1, keepdims=True)) + 1e-05) * gain_f[None]
            normed = normed.astype(jnp.bfloat16).reshape(BLOCK, HEADS * HEAD_DIM)
            out = jnp.dot(normed, w_out, preferred_element_type=jnp.float32).astype(jnp.bfloat16)
            return (new_state, out)
        init = jnp.zeros((HEADS, HEAD_DIM, STATE), jnp.float32)
        final, outs = lax.scan(step, init, blocks)
        return outs.reshape(LENGTH, outs.shape[-1])
    return lax.map(one_mixture, (tokens, log_forget_rate))
```

```python
import functools

import jax
import jax.numpy as jnp
from jax import lax
from jax.experimental import pallas as pl
from jax.experimental.pallas import tpu as pltpu
from jax.sharding import PartitionSpec as P

HEAD_DIM = 64
STATE = 64
CONV = 4
BLOCK = 128
LANES = 128
RIM = 16
MESH = pl.DeviceIdType.MESH
F32 = jnp.float32
BF16 = jnp.bfloat16


def flipped(index, bit):
    return index + bit - 2 * bit * ((index // bit) % 2)


def dot(a, b):
    return lax.dot_general(a, b, (((1,), (0,)), ((), ())), preferred_element_type=F32)


def dot_nt(a, b):
    return lax.dot_general(a, b, (((1,), (1,)), ((), ())), preferred_element_type=F32)


def split_dot(a, b):
    high = a.astype(BF16)
    low = (a - high.astype(F32)).astype(BF16)
    return dot(high, b) + dot(low, b)


def silu(x):
    return x / (1.0 + jnp.exp(-x))


def iota(shape, dim):
    return lax.broadcasted_iota(jnp.int32, shape, dim)


def one_minus_exp(x):
    total = jnp.ones_like(x)
    for k in range(14, 1, -1):
        total = 1.0 + x * (1.0 / k) * total
    return -x * total


def kernel(
    seq, mix,
    tok, rate, wx, wz, wbc, par, cbc, wo, out,
    halo, wxb, wzb, wob, parb, logs, logsrc, pre, xact, bcs, bts, cums, tails, ecs, rows_t,
    cbm, first, yloc, sgate, normed, sbuf, rbuf, cbuf, gbuf,
    bsend, brecv, fsend, hsend, hrecv, lsend, lrecv, asend, arecv, csend, crecv,
):
    me_s, me_m = lax.axis_index("seq"), lax.axis_index("mix")
    mixtures, length = tok.shape[0], tok.shape[1]
    width = wx.shape[1]
    per = width // HEAD_DIM
    heads = rate.shape[2]
    blocks = length // BLOCK
    nrows = STATE // seq
    bits = [1 << i for i in range(mix.bit_length() - 1)]

    barrier = pltpu.get_barrier_semaphore()
    for bit in bits:
        pl.semaphore_signal(barrier, inc=1, device_id={"mix": flipped(me_m, bit)}, device_id_type=MESH)

    @pl.loop(1, seq)
    def _(i):
        pl.semaphore_signal(barrier, inc=1, device_id={"seq": (me_s + i) % seq}, device_id_type=MESH)

    pl.semaphore_wait(barrier, len(bits) + seq - 1)

    shards = ((wx, wxb), (par, parb), (wz, wzb), (wo, wob))

    def held(which, offset):
        own, slots = shards[which]
        return own if offset == 0 else slots.at[offset - 1]

    def share(which, offset, bit):
        slot = shards[which][1].at[offset + bit - 1]
        return pltpu.make_async_remote_copy(
            src_ref=held(which, offset), dst_ref=slot,
            send_sem=bsend.at[which, offset + bit - 1], recv_sem=brecv.at[which, offset + bit - 1],
            device_id={"mix": flipped(me_m, bit)}, device_id_type=MESH,
        )

    def low_bit(offset):
        return offset & -offset

    def arrived(which, offset):
        share(which, offset - low_bit(offset), low_bit(offset)).wait_recv()
        for bit in bits:
            if bit < low_bit(offset):
                share(which, offset, bit).start()

    rim_copy = pltpu.make_async_remote_copy(
        src_ref=tok.at[:, pl.ds(length - RIM, RIM), :], dst_ref=halo,
        send_sem=hsend, recv_sem=hrecv,
        device_id={"seq": (me_s + 1) % seq}, device_id_type=MESH,
    )
    rim_copy.start()
    for which in (1, 0, 2, 3):
        for bit in reversed(bits):
            share(which, 0, bit).start()

    here = iota((heads, LANES), 0)
    there = iota((heads, LANES), 1)
    order = jnp.zeros((heads, LANES), jnp.bool_)
    for offset in range(mix):
        actual = me_m
        for bit in bits:
            if offset & bit:
                actual = flipped(actual, bit)
        order = order | ((there // per == offset) & (here == actual * per + there % per))
    order = order.astype(F32).astype(BF16)
    lower = (iota((BLOCK, BLOCK), 0) >= iota((BLOCK, BLOCK), 1)).astype(F32)
    lower_b = lower.astype(BF16)

    totals = []
    for m in range(mixtures):
        device_total = jnp.zeros((1, LANES), F32)
        for b in range(blocks):
            at = pl.ds(b * BLOCK, BLOCK)
            mine = dot(rate[m, at, :], order)
            cum = dot(lower_b, mine.astype(BF16))
            gain_in = jnp.sqrt(one_minus_exp(2.0 * mine))
            last = cum[BLOCK - 1 : BLOCK]
            cums[m, at, :] = cum
            ecs[m, at, :] = jnp.exp(cum)
            tails[m, at, :] = jnp.exp(last - cum) * gain_in
            rows_t[m * blocks + b] = jnp.transpose(cum - jnp.log(gain_in))
            device_total = device_total + last
            totals.append(last)
        logsrc[pl.ds(m, 1), :] = device_total
    logsrc[pl.ds(mixtures, 8 - mixtures), :] = jnp.zeros((8 - mixtures, LANES), F32)
    logs[me_s] = logsrc[...]

    def log_copy(peer):
        return pltpu.make_async_remote_copy(
            src_ref=logsrc, dst_ref=logs.at[me_s], send_sem=lsend, recv_sem=lrecv,
            device_id={"seq": peer}, device_id_type=MESH,
        )

    @pl.loop(1, seq)
    def _(i):
        log_copy((me_s + i) % seq).start()

    inside = jnp.where(me_s > 0, 1.0, 0.0)

    def convolve(weight, taps, m, columns):
        total = jnp.zeros((length, columns), F32)
        for k in range(CONV):
            total = total + taps[k : k + 1].astype(F32) * pre[
                m, pl.ds(8 - CONV + 1 + k, length), pl.ds(0, columns)
            ]
        return silu(total)

    def project(weight, m, columns):
        edge = dot(halo[m], weight).astype(BF16).astype(F32)
        pre[m, pl.ds(0, 8), pl.ds(0, columns)] = edge[RIM - 8 :] * inside
        pre[m, pl.ds(8, length), pl.ds(0, columns)] = dot(tok[m], weight).astype(BF16).astype(F32)

    rim_copy.wait_recv()
    for m in range(mixtures):
        project(wbc[...], m, 2 * STATE)
        bc = convolve(None, cbc[...], m, 2 * STATE)
        bcs[m] = bc.astype(BF16)
        for b in range(blocks):
            part = bc[b * BLOCK : (b + 1) * BLOCK].astype(BF16)
            bts[m * blocks + b] = jnp.transpose(part.astype(F32))[:STATE].astype(BF16)
            scores = dot_nt(part[:, STATE:], part[:, :STATE])
            cbm[m * blocks + b] = scores * lower

    def spread(offset):
        return (iota((LANES, width), 0) == offset * per + iota((LANES, width), 1) // HEAD_DIM).astype(F32).astype(BF16)

    def states(offset):
        weight, params, expand = held(0, offset)[...], held(1, offset)[...], spread(offset)
        lanes = pl.ds(offset * width, width)
        per_mixture = []
        for m in range(mixtures):
            project(weight, m, width)
            x_act = convolve(None, params, m, width).astype(BF16)
            xact[m, :, lanes] = x_act
            scaled = (x_act.astype(F32) * split_dot(tails[m], expand)).astype(BF16)
            state = None
            for b in range(blocks):
                new = dot(bts[m * blocks + b], scaled[b * BLOCK : (b + 1) * BLOCK])
                if b == 0:
                    state = new
                else:
                    first[m * blocks + b - 1, :, lanes] = state
                    fade = split_dot(jnp.broadcast_to(jnp.exp(totals[m * blocks + b]), (8, LANES)), expand)[:1]
                    state = fade * state + new
            per_mixture.append(state)
        for k in range(seq):
            piece = jnp.concatenate([s[k * nrows : (k + 1) * nrows] for s in per_mixture], axis=0)
            sbuf[offset, k] = piece.astype(BF16)
        rbuf[offset, me_s] = sbuf[offset, me_s]

        @pl.loop(1, seq)
        def _(i):
            state_copy(offset, (me_s + i) % seq).start()

    def state_copy(offset, peer):
        return pltpu.make_async_remote_copy(
            src_ref=sbuf.at[offset, peer], dst_ref=rbuf.at[offset, me_s],
            send_sem=asend.at[offset], recv_sem=arecv.at[offset],
            device_id={"seq": peer}, device_id_type=MESH,
        )

    def carry_copy(offset, peer):
        return pltpu.make_async_remote_copy(
            src_ref=cbuf.at[offset, peer], dst_ref=gbuf.at[offset, me_s],
            send_sem=csend.at[offset], recv_sem=crecv.at[offset],
            device_id={"seq": peer}, device_id_type=MESH,
        )

    def wait_all(ref, sem):
        some = ref.at[pl.ds(0, seq - 1)]
        pltpu.make_async_copy(some, some, sem).wait()

    def carries(offset):
        wait_all(rbuf.at[offset], arecv.at[offset])
        expand = spread(offset)
        fade = split_dot(jnp.exp(logs[...].reshape(seq * 8, LANES)), expand)
        carry = jnp.zeros((mixtures * nrows, width), F32)
        for p in range(seq):
            cbuf[offset, p] = carry.astype(BF16)
            if p < seq - 1:
                down = jnp.concatenate(
                    [jnp.broadcast_to(fade[p * 8 + m : p * 8 + m + 1], (nrows, width)) for m in range(mixtures)], axis=0
                )
                carry = down * carry + rbuf[offset, p].astype(F32)
        gbuf[offset, me_s] = cbuf[offset, me_s]

        @pl.loop(1, seq)
        def _(i):
            carry_copy(offset, (me_s + i) % seq).start()

    group_of = iota((BLOCK, width), 1) // HEAD_DIM

    def intra(offset):
        lanes = pl.ds(offset * width, width)
        skip_row = held(1, offset)[pl.ds(CONV + 1, 1), :].astype(F32)
        for m in range(mixtures):
            for b in range(blocks):
                at = pl.ds(b * BLOCK, BLOCK)
                scores = cbm[m * blocks + b]
                cum = cums[m, at, :]
                parts = []
                for i in range(per):
                    j = offset * per + i
                    gap = cum[:, j : j + 1] - rows_t[m * blocks + b, pl.ds(j, 1), :]
                    parts.append((jnp.exp(jnp.minimum(gap, 0.0)) * scores).astype(BF16))
                x_act = xact[m, at, lanes]
                full = dot(jnp.concatenate(parts, axis=0), x_act)
                total = full[:BLOCK]
                for i in range(1, per):
                    total = jnp.where(group_of == i, full[i * BLOCK : (i + 1) * BLOCK], total)
                yloc[m, at, lanes] = total + skip_row * x_act.astype(F32)

    def gate(offset):
        lanes = pl.ds(offset * width, width)
        weight = held(2, offset)[...]
        for m in range(mixtures):
            sgate[m, :, lanes] = silu(dot(tok[m], weight).astype(BF16).astype(F32))

    same_head = (iota((width, width), 0) // HEAD_DIM == iota((width, width), 1) // HEAD_DIM).astype(F32).astype(BF16)

    def finish(offset):
        lanes = pl.ds(offset * width, width)
        wait_all(gbuf.at[offset], crecv.at[offset])
        expand = spread(offset)
        gain_row = held(1, offset)[pl.ds(CONV, 1), :].astype(F32)
        for m in range(mixtures):
            state = jnp.concatenate(
                [gbuf[offset, k].astype(F32)[m * nrows : (m + 1) * nrows] for k in range(seq)], axis=0
            )
            grow = split_dot(ecs[m], expand)
            for b in range(blocks):
                at = pl.ds(b * BLOCK, BLOCK)
                if b > 0:
                    fade = split_dot(jnp.broadcast_to(jnp.exp(totals_sum(m, b)), (8, LANES)), expand)[:1]
                    incoming = fade * state + first[m * blocks + b - 1, :, lanes]
                else:
                    incoming = state
                inter = dot(bcs[m, at, :][:, STATE:], incoming.astype(BF16))
                y = yloc[m, at, lanes] + grow[b * BLOCK : (b + 1) * BLOCK] * inter
                v = y * sgate[m, at, lanes]
                power = split_dot(v * v, same_head) * (1.0 / HEAD_DIM)
                normed[m, at, lanes] = (v * lax.rsqrt(power + 1e-05) * gain_row).astype(BF16)

    def totals_sum(m, b):
        total = totals[m * blocks]
        for k in range(1, b):
            total = total + totals[m * blocks + k]
        return total

    def take(which, offset):
        if offset:
            arrived(which, offset)

    for offset in range(mix):
        take(1, offset)
        take(0, offset)
        states(offset)
        if offset == 0:
            intra(offset)
    pltpu.make_async_copy(logs.at[pl.ds(0, seq - 1)], logs.at[pl.ds(0, seq - 1)], lrecv).wait()
    for offset in range(mix):
        carries(offset)
        take(2, offset)
        gate(offset)
    for offset in range(1, mix):
        intra(offset)
        take(3, offset)
    for offset in range(mix):
        finish(offset)
    for m in range(mixtures):
        total = jnp.zeros((length, wo.shape[1]), F32)
        for offset in range(mix):
            total = total + dot(normed[m, :, pl.ds(offset * width, width)], held(3, offset)[...])
        out[m] = total.astype(BF16)

    rim_copy.wait_send()
    for which in range(4):
        for offset in range(mix):
            for bit in bits:
                if offset == 0 or bit < low_bit(offset):
                    share(which, offset, bit).wait_send()
    wait_all(logs, lsend)
    for offset in range(mix):
        wait_all(sbuf.at[offset], asend.at[offset])
        wait_all(cbuf.at[offset], csend.at[offset])


def solution(mesh):
    seq, mix = mesh.shape["seq"], mesh.shape["mix"]

    def body(tokens, log_forget_rate, w_x, w_z, w_bc, conv_x, conv_bc, skip, gain, w_out):
        mixtures, length, depth = tokens.shape
        width = w_x.shape[1]
        inner = width * mix
        blocks = length // BLOCK
        params = jnp.concatenate(
            [
                conv_x,
                gain[None],
                jnp.repeat(skip, HEAD_DIM)[None],
                jnp.zeros((16 - CONV - 2, width), BF16),
            ],
            axis=0,
        )
        vmem = pl.BlockSpec(memory_space=pltpu.VMEM)
        dma = pltpu.SemaphoreType.DMA
        rows = mixtures * (STATE // seq)
        return pl.pallas_call(
            functools.partial(kernel, seq, mix),
            out_shape=jax.ShapeDtypeStruct((mixtures, length, w_out.shape[1]), BF16),
            in_specs=[vmem] * 8,
            out_specs=vmem,
            scratch_shapes=[
                pltpu.VMEM((mixtures, RIM, depth), BF16),
                pltpu.VMEM((mix - 1,) + w_x.shape, BF16),
                pltpu.VMEM((mix - 1,) + w_z.shape, BF16),
                pltpu.VMEM((mix - 1,) + w_out.shape, BF16),
                pltpu.VMEM((mix - 1, 16, width), BF16),
                pltpu.VMEM((seq, 8, LANES), F32),
                pltpu.VMEM((8, LANES), F32),
                pltpu.VMEM((mixtures, 8 + length, width), F32),
                pltpu.VMEM((mixtures, length, inner), BF16),
                pltpu.VMEM((mixtures, length, 2 * STATE), BF16),
                pltpu.VMEM((mixtures * blocks, STATE, BLOCK), BF16),
                pltpu.VMEM((mixtures, length, LANES), F32),
                pltpu.VMEM((mixtures, length, LANES), F32),
                pltpu.VMEM((mixtures, length, LANES), F32),
                pltpu.VMEM((mixtures * blocks, LANES, BLOCK), F32),
                pltpu.VMEM((mixtures * blocks, BLOCK, BLOCK), F32),
                pltpu.VMEM((mixtures * blocks, STATE, inner), F32),
                pltpu.VMEM((mixtures, length, inner), F32),
                pltpu.VMEM((mixtures, length, inner), F32),
                pltpu.VMEM((mixtures, length, inner), BF16),
                pltpu.VMEM((mix, seq, rows, width), BF16),
                pltpu.VMEM((mix, seq, rows, width), BF16),
                pltpu.VMEM((mix, seq, rows, width), BF16),
                pltpu.VMEM((mix, seq, rows, width), BF16),
                dma((4, mix - 1)),
                dma((4, mix - 1)),
                dma,
                dma,
                dma,
                dma,
                dma,
                dma((mix,)),
                dma((mix,)),
                dma((mix,)),
                dma((mix,)),
            ],
            compiler_params=pltpu.CompilerParams(
                collective_id=0, has_side_effects=True, vmem_limit_bytes=56 * 1024 * 1024
            ),
        )(tokens, log_forget_rate, w_x, w_z, w_bc, params, conv_bc, w_out)

    return jax.shard_map(
        body,
        mesh=mesh,
        in_specs=(
            P("mix", "seq", None),
            P("mix", "seq", None),
            P(None, "mix"),
            P(None, "mix"),
            P(),
            P(None, "mix"),
            P(),
            P("mix"),
            P("mix"),
            P("mix", None),
        ),
        out_specs=P("mix", "seq", None),
        check_vma=False,
    )
```

```python
import functools

import jax
import jax.numpy as jnp
from jax import lax
from jax.experimental import pallas as pl
from jax.experimental.pallas import tpu as pltpu
from jax.sharding import PartitionSpec as P

HEAD_DIM = 64
STATE = 64
CONV = 4
BLOCK = 128
LANES = 128
RIM = 16
MESH = pl.DeviceIdType.MESH
F32 = jnp.float32
BF16 = jnp.bfloat16


def flipped(index, bit):
    return index + bit - 2 * bit * ((index // bit) % 2)


def dot(a, b):
    return lax.dot_general(a, b, (((1,), (0,)), ((), ())), preferred_element_type=F32)


def dot_nt(a, b):
    return lax.dot_general(a, b, (((1,), (1,)), ((), ())), preferred_element_type=F32)


def split_dot(a, b):
    high = a.astype(BF16)
    low = (a - high.astype(F32)).astype(BF16)
    return dot(high, b) + dot(low, b)


def silu(x):
    return x / (1.0 + jnp.exp(-x))


def iota(shape, dim):
    return lax.broadcasted_iota(jnp.int32, shape, dim)


def one_minus_exp(x):
    total = jnp.ones_like(x)
    for k in range(14, 1, -1):
        total = 1.0 + x * (1.0 / k) * total
    return -x * total


def kernel(
    seq, mix,
    tok_in, rate, wx_in, wz_in, wbc, cx, cbc, skip, gain, wo_in, out,
    tok, wx, wz, wo, par, halo, wxb, wzb, wob, parb, logs, logsrc, pre, xact, bcs, bts, cums, tails, ecs, rows_t,
    cbm, first, yloc, sgate, normed, sbuf, rbuf, cbuf, gbuf,
    loads, bsend, brecv, xsend, xrecv, ysend, yrecv, fsend, hsend, hrecv, lsend, lrecv, asend, arecv, csend, crecv,
):
    me_s, me_m = lax.axis_index("seq"), lax.axis_index("mix")
    mixtures, length = tok.shape[0], tok.shape[1]
    width = wx.shape[2]
    per = width // HEAD_DIM
    heads = rate.shape[1]
    blocks = length // BLOCK
    nrows = STATE // seq
    bits = [1 << i for i in range(mix.bit_length() - 1)]

    local = [
        pltpu.make_async_copy(src, dst, loads.at[i])
        for i, (src, dst) in enumerate(((wx_in, wx), (tok_in, tok), (wz_in, wz), (wo_in, wo)))
    ]
    for copy in local:
        copy.start()

    barrier = pltpu.get_barrier_semaphore()
    for bit in bits:
        pl.semaphore_signal(barrier, inc=1, device_id={"mix": flipped(me_m, bit)}, device_id_type=MESH)

    @pl.loop(1, seq)
    def _(i):
        pl.semaphore_signal(barrier, inc=1, device_id={"seq": (me_s + i) % seq}, device_id_type=MESH)

    lane_head = iota((8, width), 1) // HEAD_DIM
    skip_row = jnp.zeros((8, width), F32)
    skip_in = jnp.broadcast_to(skip[...].astype(F32)[None, :], (8, per))
    for i in range(per):
        skip_row = jnp.where(lane_head == i, skip_in[:, i : i + 1], skip_row)
    gain_in = jnp.broadcast_to(gain[...].astype(F32)[None, :], (8, width))
    place = iota((16 - CONV * 2, width), 0)
    par[pl.ds(0, CONV), :] = cx[...]
    par[pl.ds(CONV * 2, 16 - CONV * 2), :] = jnp.where(place == 0, gain_in, skip_row).astype(BF16)
    par[pl.ds(CONV, CONV), :] = jnp.zeros((CONV, width), BF16)
    pl.semaphore_wait(barrier, len(bits) + seq - 1)

    shards = ((wx, wxb), (par, parb), (wz, wzb), (wo, wob))

    def held(which, offset):
        own, slots = shards[which]
        return own if offset == 0 else slots.at[offset - 1]

    def share(which, offset, bit):
        slot = shards[which][1].at[offset + bit - 1]
        return pltpu.make_async_remote_copy(
            src_ref=held(which, offset), dst_ref=slot,
            send_sem=bsend.at[which, offset + bit - 1], recv_sem=brecv.at[which, offset + bit - 1],
            device_id={"mix": flipped(me_m, bit)}, device_id_type=MESH,
        )

    def low_bit(offset):
        return offset & -offset

    top = bits[-1]
    half, other = me_s % 2, 1 - me_s % 2

    def cross(which):
        own, slots = shards[which]
        return pltpu.make_async_remote_copy(
            src_ref=own.at[half], dst_ref=slots.at[top - 1, half],
            send_sem=xsend.at[which - 2], recv_sem=xrecv.at[which - 2],
            device_id={"mix": flipped(me_m, top)}, device_id_type=MESH,
        )

    def beside(which, part):
        slots = shards[which][1]
        return pltpu.make_async_remote_copy(
            src_ref=slots.at[top - 1, part], dst_ref=slots.at[top - 1, part],
            send_sem=ysend.at[which - 2], recv_sem=yrecv.at[which - 2],
            device_id={"seq": flipped(me_s, 1)}, device_id_type=MESH,
        )

    def is_split(which, offset):
        return which >= 2 and offset == top

    def crossed(which):
        cross(which).wait_recv()
        beside(which, half).start()

    def arrived(which, offset):
        if is_split(which, offset):
            beside(which, other).wait_recv()
        else:
            share(which, offset - low_bit(offset), low_bit(offset)).wait_recv()
        for bit in bits:
            if bit < low_bit(offset):
                share(which, offset, bit).start()

    rim_copy = pltpu.make_async_remote_copy(
        src_ref=tok.at[:, pl.ds(length - RIM, RIM), :], dst_ref=halo,
        send_sem=hsend, recv_sem=hrecv,
        device_id={"seq": (me_s + 1) % seq}, device_id_type=MESH,
    )
    local[0].wait()
    for which in (0, 1):
        for bit in reversed(bits):
            share(which, 0, bit).start()
    local[1].wait()

    @pl.when(me_s < seq - 1)
    def _():
        rim_copy.start()

    @pl.when(me_s == 0)
    def _():
        halo[...] = jnp.zeros_like(halo)

    for which in (2, 3):
        local[which].wait()
        cross(which).start()
        for bit in bits[:-1]:
            share(which, 0, bit).start()

    here = iota((LANES, heads), 1)
    there = iota((LANES, heads), 0)
    order = jnp.zeros((LANES, heads), jnp.bool_)
    for offset in range(mix):
        actual = me_m
        for bit in bits:
            if offset & bit:
                actual = flipped(actual, bit)
        order = order | ((there // per == offset) & (here == actual * per + there % per))
    order = order.astype(F32).astype(BF16)
    lower = (iota((BLOCK, BLOCK), 0) >= iota((BLOCK, BLOCK), 1)).astype(F32)
    upper_b = jnp.transpose(lower).astype(BF16)

    totals = []
    for m in range(mixtures):
        device_total = jnp.zeros((1, LANES), F32)
        for b in range(blocks):
            at = pl.ds(b * BLOCK, BLOCK)
            mine = dot(order, rate[m, :, b * BLOCK : (b + 1) * BLOCK])[: heads]
            cum = dot(mine.astype(BF16), upper_b)
            gain_log = jnp.log(jnp.sqrt(one_minus_exp(2.0 * mine)))
            gain_in = jnp.sqrt(one_minus_exp(2.0 * mine))
            tail = jnp.exp(cum[:, BLOCK - 1 :] - cum) * gain_in
            rows_t[m * blocks + b, pl.ds(0, heads), :] = cum - gain_log
            blank = jnp.zeros((LANES - heads, BLOCK), F32)
            cum_t = jnp.transpose(jnp.concatenate([cum, blank], axis=0))
            cums[m, at, :] = cum_t
            ecs[m, at, :] = jnp.exp(cum_t)
            tails[m, at, :] = jnp.transpose(jnp.concatenate([tail, blank], axis=0))
            last = cum_t[BLOCK - 1 :]
            device_total = device_total + last
            totals.append(last)
        logsrc[pl.ds(m, 1), :] = device_total
    logsrc[pl.ds(mixtures, 8 - mixtures), :] = jnp.zeros((8 - mixtures, LANES), F32)
    logs[me_s] = logsrc[...]

    def log_copy(peer):
        return pltpu.make_async_remote_copy(
            src_ref=logsrc, dst_ref=logs.at[me_s], send_sem=lsend, recv_sem=lrecv,
            device_id={"seq": peer}, device_id_type=MESH,
        )

    @pl.loop(1, seq)
    def _(i):
        log_copy((me_s + i) % seq).start()

    def convolve(weight, taps, m, columns):
        total = jnp.zeros((length, columns), F32)
        for k in range(CONV):
            total = total + taps[k : k + 1].astype(F32) * pre[
                m, pl.ds(8 - CONV + 1 + k, length), pl.ds(0, columns)
            ]
        return silu(total)

    def project(weight, m, columns):
        edge = dot(halo[m], weight).astype(BF16).astype(F32)
        pre[m, pl.ds(0, 8), pl.ds(0, columns)] = edge[RIM - 8 :]
        pre[m, pl.ds(8, length), pl.ds(0, columns)] = dot(tok[m], weight).astype(BF16).astype(F32)

    @pl.when(me_s > 0)
    def _():
        rim_copy.wait_recv()

    for m in range(mixtures):
        project(wbc[...], m, 2 * STATE)
        bc = convolve(None, cbc[...], m, 2 * STATE)
        bcs[m] = bc.astype(BF16)
        for b in range(blocks):
            part = bc[b * BLOCK : (b + 1) * BLOCK].astype(BF16)
            bts[m * blocks + b] = jnp.transpose(part.astype(F32))[:STATE].astype(BF16)
            scores = dot_nt(part[:, STATE:], part[:, :STATE])
            cbm[m * blocks + b] = scores * lower

    def flat(weight):
        return weight.reshape(weight.shape[0] * weight.shape[1], weight.shape[2])

    def spread(offset):
        return (iota((LANES, width), 0) == offset * per + iota((LANES, width), 1) // HEAD_DIM).astype(F32).astype(BF16)

    def states(offset):
        weight, params, expand = flat(held(0, offset)[...]), held(1, offset)[...], spread(offset)
        lanes = pl.ds(offset * width, width)
        per_mixture = []
        for m in range(mixtures):
            project(weight, m, width)
            x_act = convolve(None, params, m, width).astype(BF16)
            xact[m, :, lanes] = x_act
            scaled = (x_act.astype(F32) * split_dot(tails[m], expand)).astype(BF16)
            state = None
            for b in range(blocks):
                new = dot(bts[m * blocks + b], scaled[b * BLOCK : (b + 1) * BLOCK])
                if b == 0:
                    state = new
                else:
                    first[m * blocks + b - 1, :, lanes] = state
                    fade = split_dot(jnp.broadcast_to(jnp.exp(totals[m * blocks + b]), (8, LANES)), expand)[:1]
                    state = fade * state + new
            per_mixture.append(state)
        for k in range(seq):
            piece = jnp.concatenate([s[k * nrows : (k + 1) * nrows] for s in per_mixture], axis=0)
            sbuf[offset, k] = piece.astype(BF16)
        rbuf[offset, me_s] = sbuf[offset, me_s]

        @pl.loop(1, seq)
        def _(i):
            state_copy(offset, (me_s + i) % seq).start()

    def state_copy(offset, peer):
        return pltpu.make_async_remote_copy(
            src_ref=sbuf.at[offset, peer], dst_ref=rbuf.at[offset, me_s],
            send_sem=asend.at[offset], recv_sem=arecv.at[offset],
            device_id={"seq": peer}, device_id_type=MESH,
        )

    def carry_copy(offset, peer):
        return pltpu.make_async_remote_copy(
            src_ref=cbuf.at[offset, peer], dst_ref=gbuf.at[offset, me_s],
            send_sem=csend.at[offset], recv_sem=crecv.at[offset],
            device_id={"seq": peer}, device_id_type=MESH,
        )

    def wait_all(ref, sem):
        some = ref.at[pl.ds(0, seq - 1)]
        pltpu.make_async_copy(some, some, sem).wait()

    def carries(offset):
        wait_all(rbuf.at[offset], arecv.at[offset])
        expand = spread(offset)
        fade = split_dot(jnp.exp(logs[...].reshape(seq * 8, LANES)), expand)
        carry = jnp.zeros((mixtures * nrows, width), F32)
        for p in range(seq):
            cbuf[offset, p] = carry.astype(BF16)
            if p < seq - 1:
                down = jnp.concatenate(
                    [jnp.broadcast_to(fade[p * 8 + m : p * 8 + m + 1], (nrows, width)) for m in range(mixtures)], axis=0
                )
                carry = down * carry + rbuf[offset, p].astype(F32)
        gbuf[offset, me_s] = cbuf[offset, me_s]

        @pl.loop(1, seq)
        def _(i):
            carry_copy(offset, (me_s + i) % seq).start()

    group_of = iota((BLOCK, width), 1) // HEAD_DIM

    def intra(offset):
        lanes = pl.ds(offset * width, width)
        skip_row = held(1, offset)[pl.ds(CONV * 2 + 1, 1), :].astype(F32)
        for m in range(mixtures):
            for b in range(blocks):
                at = pl.ds(b * BLOCK, BLOCK)
                scores = cbm[m * blocks + b]
                cum = cums[m, at, :]
                parts = []
                for i in range(per):
                    j = offset * per + i
                    gap = cum[:, j : j + 1] - rows_t[m * blocks + b, pl.ds(j, 1), :]
                    parts.append((jnp.exp(jnp.minimum(gap, 0.0)) * scores).astype(BF16))
                x_act = xact[m, at, lanes]
                full = dot(jnp.concatenate(parts, axis=0), x_act)
                total = full[:BLOCK]
                for i in range(1, per):
                    total = jnp.where(group_of == i, full[i * BLOCK : (i + 1) * BLOCK], total)
                yloc[m, at, lanes] = total + skip_row * x_act.astype(F32)

    def gate(offset):
        lanes = pl.ds(offset * width, width)
        weight = flat(held(2, offset)[...])
        for m in range(mixtures):
            sgate[m, :, lanes] = silu(dot(tok[m], weight).astype(BF16).astype(F32))

    same_head = (iota((width, width), 0) // HEAD_DIM == iota((width, width), 1) // HEAD_DIM).astype(F32).astype(BF16)

    def finish(offset):
        lanes = pl.ds(offset * width, width)
        wait_all(gbuf.at[offset], crecv.at[offset])
        expand = spread(offset)
        gain_row = held(1, offset)[pl.ds(CONV * 2, 1), :].astype(F32)
        for m in range(mixtures):
            state = jnp.concatenate(
                [gbuf[offset, k].astype(F32)[m * nrows : (m + 1) * nrows] for k in range(seq)], axis=0
            )
            grow = split_dot(ecs[m], expand)
            for b in range(blocks):
                at = pl.ds(b * BLOCK, BLOCK)
                if b > 0:
                    fade = split_dot(jnp.broadcast_to(jnp.exp(totals_sum(m, b)), (8, LANES)), expand)[:1]
                    incoming = fade * state + first[m * blocks + b - 1, :, lanes]
                else:
                    incoming = state
                inter = dot(bcs[m, at, :][:, STATE:], incoming.astype(BF16))
                y = yloc[m, at, lanes] + grow[b * BLOCK : (b + 1) * BLOCK] * inter
                v = y * sgate[m, at, lanes]
                power = split_dot(v * v, same_head) * (1.0 / HEAD_DIM)
                normed[m, at, lanes] = (v * lax.rsqrt(power + 1e-05) * gain_row).astype(BF16)

    def totals_sum(m, b):
        total = totals[m * blocks]
        for k in range(1, b):
            total = total + totals[m * blocks + k]
        return total

    def take(which, offset):
        if offset:
            arrived(which, offset)

    def logs_arrived():
        some = logs.at[pl.ds(0, seq - 1)]
        pltpu.make_async_copy(some, some, lrecv).wait()

    for offset in range(top):
        take(1, offset)
        take(0, offset)
        states(offset)
        intra(offset)
    for offset in range(top):
        take(2, offset)
        gate(offset)
    for offset in range(top, mix):
        take(1, offset)
        take(0, offset)
        states(offset)
    logs_arrived()
    for offset in range(top):
        carries(offset)
        take(3, offset)
    crossed(2)
    for offset in range(top, mix):
        intra(offset)
        if offset == top:
            carries(offset)
            crossed(3)
    take(2, top)
    for offset in range(top + 1, mix):
        carries(offset)
    finish(0)
    gate(top)
    take(3, top)
    for offset in range(1, top):
        finish(offset)
    for offset in range(top + 1, mix):
        take(2, offset)
        gate(offset)
    for offset in range(top, mix):
        finish(offset)
        if offset > top:
            take(3, offset)
    for m in range(mixtures):
        total = jnp.zeros((length, wo.shape[2]), F32)
        for offset in range(mix):
            total = total + dot(normed[m, :, pl.ds(offset * width, width)], flat(held(3, offset)[...]))
        out[m] = total.astype(BF16)

    @pl.when(me_s < seq - 1)
    def _():
        rim_copy.wait_send()

    for which in range(4):
        for offset in range(mix):
            for bit in bits:
                if (offset == 0 or bit < low_bit(offset)) and not is_split(which, offset + bit):
                    share(which, offset, bit).wait_send()
    for which in (2, 3):
        cross(which).wait_send()
        beside(which, half).wait_send()
    wait_all(logs, lsend)
    for offset in range(mix):
        wait_all(sbuf.at[offset], asend.at[offset])
        wait_all(cbuf.at[offset], csend.at[offset])


def solution(mesh):
    seq, mix = mesh.shape["seq"], mesh.shape["mix"]

    def body(tokens, log_forget_rate, w_x, w_z, w_bc, conv_x, conv_bc, skip, gain, w_out):
        mixtures, length, depth = tokens.shape
        width = w_x.shape[1]
        rate = jnp.transpose(log_forget_rate, (0, 2, 1))
        inner = width * mix
        blocks = length // BLOCK
        w_x, w_z, w_out = (w.reshape(2, w.shape[0] // 2, w.shape[1]) for w in (w_x, w_z, w_out))
        vmem = pl.BlockSpec(memory_space=pltpu.VMEM)
        hbm = pl.BlockSpec(memory_space=pl.ANY)
        dma = pltpu.SemaphoreType.DMA
        rows = mixtures * (STATE // seq)
        return pl.pallas_call(
            functools.partial(kernel, seq, mix),
            out_shape=jax.ShapeDtypeStruct((mixtures, length, w_out.shape[2]), BF16),
            in_specs=[hbm, vmem, hbm, hbm, vmem, vmem, vmem, vmem, vmem, hbm],
            out_specs=vmem,
            scratch_shapes=[
                pltpu.VMEM(tokens.shape, BF16),
                pltpu.VMEM(w_x.shape, BF16),
                pltpu.VMEM(w_z.shape, BF16),
                pltpu.VMEM(w_out.shape, BF16),
                pltpu.VMEM((16, width), BF16),
                pltpu.VMEM((mixtures, RIM, depth), BF16),
                pltpu.VMEM((mix - 1,) + w_x.shape, BF16),
                pltpu.VMEM((mix - 1,) + w_z.shape, BF16),
                pltpu.VMEM((mix - 1,) + w_out.shape, BF16),
                pltpu.VMEM((mix - 1, 16, width), BF16),
                pltpu.VMEM((seq, 8, LANES), F32),
                pltpu.VMEM((8, LANES), F32),
                pltpu.VMEM((mixtures, 8 + length, width), F32),
                pltpu.VMEM((mixtures, length, inner), BF16),
                pltpu.VMEM((mixtures, length, 2 * STATE), BF16),
                pltpu.VMEM((mixtures * blocks, STATE, BLOCK), BF16),
                pltpu.VMEM((mixtures, length, LANES), F32),
                pltpu.VMEM((mixtures, length, LANES), F32),
                pltpu.VMEM((mixtures, length, LANES), F32),
                pltpu.VMEM((mixtures * blocks, LANES, BLOCK), F32),
                pltpu.VMEM((mixtures * blocks, BLOCK, BLOCK), F32),
                pltpu.VMEM((mixtures * blocks, STATE, inner), F32),
                pltpu.VMEM((mixtures, length, inner), F32),
                pltpu.VMEM((mixtures, length, inner), F32),
                pltpu.VMEM((mixtures, length, inner), BF16),
                pltpu.VMEM((mix, seq, rows, width), BF16),
                pltpu.VMEM((mix, seq, rows, width), BF16),
                pltpu.VMEM((mix, seq, rows, width), BF16),
                pltpu.VMEM((mix, seq, rows, width), BF16),
                dma((4,)),
                dma((4, mix - 1)),
                dma((4, mix - 1)),
                dma((2,)),
                dma((2,)),
                dma((2,)),
                dma((2,)),
                dma,
                dma,
                dma,
                dma,
                dma,
                dma((mix,)),
                dma((mix,)),
                dma((mix,)),
                dma((mix,)),
            ],
            compiler_params=pltpu.CompilerParams(
                collective_id=0, has_side_effects=True, vmem_limit_bytes=40 * 1024 * 1024
            ),
        )(tokens, rate, w_x, w_z, w_bc, conv_x, conv_bc, skip, gain, w_out)

    return jax.shard_map(
        body,
        mesh=mesh,
        in_specs=(
            P("mix", "seq", None),
            P("mix", "seq", None),
            P(None, "mix"),
            P(None, "mix"),
            P(),
            P(None, "mix"),
            P(),
            P("mix"),
            P("mix"),
            P("mix", None),
        ),
        out_specs=P("mix", "seq", None),
        check_vma=False,
    )
```

```python
import functools

import jax
import jax.numpy as jnp
from jax import lax
from jax.experimental import pallas as pl
from jax.experimental.pallas import tpu as pltpu
from jax.sharding import PartitionSpec as P

HEAD_DIM = 64
STATE = 64
CONV = 4
BLOCK = 128
LANES = 128
RIM = 16
MESH = pl.DeviceIdType.MESH
F32 = jnp.float32
BF16 = jnp.bfloat16


def flipped(index, bit):
    return index + bit - 2 * bit * ((index // bit) % 2)


def dot(a, b):
    return lax.dot_general(a, b, (((1,), (0,)), ((), ())), preferred_element_type=F32)


def dot_nt(a, b):
    return lax.dot_general(a, b, (((1,), (1,)), ((), ())), preferred_element_type=F32)


def split_dot(a, b):
    high = a.astype(BF16)
    low = (a - high.astype(F32)).astype(BF16)
    return dot(high, b) + dot(low, b)


def silu(x):
    return x / (1.0 + jnp.exp(-x))


def iota(shape, dim):
    return lax.broadcasted_iota(jnp.int32, shape, dim)


def one_minus_exp(x):
    total = jnp.ones_like(x)
    for k in range(14, 1, -1):
        total = 1.0 + x * (1.0 / k) * total
    return -x * total


def kernel(
    seq, mix,
    tok_in, rate_in, wx_in, wz_in, wbc_in, cx_in, cbc_in, skip_in, gain_in, wo_in, out,
    tok, rate, wx, wz, wbc, cx, cbc, skip, gain, wo, par, halo, wxb, wzb, wob, parb, logs, logsrc, pre, xact, bcs, bts, cums, tails, ecs, rows_t,
    cbm, first, yloc, sgate, normed, sbuf, rbuf, cbuf, gbuf,
    loads, bsend, brecv, xsend, xrecv, ysend, yrecv, fsend, hsend, hrecv, lsend, lrecv, asend, arecv, csend, crecv,
):
    me_s, me_m = lax.axis_index("seq"), lax.axis_index("mix")
    mixtures, length = tok.shape[0], tok.shape[1]
    width = wx.shape[2]
    per = width // HEAD_DIM
    heads = rate.shape[1]
    blocks = length // BLOCK
    nrows = STATE // seq
    bits = [1 << i for i in range(mix.bit_length() - 1)]

    local = [
        pltpu.make_async_copy(src, dst, loads.at[i])
        for i, (src, dst) in enumerate(
            (
                (wx_in, wx), (tok_in, tok), (wz_in, wz), (wo_in, wo), (cx_in, cx),
                (skip_in, skip), (gain_in, gain), (rate_in, rate), (wbc_in, wbc), (cbc_in, cbc),
            )
        )
    ]
    for copy in local:
        copy.start()

    barrier = pltpu.get_barrier_semaphore()
    for bit in bits:
        pl.semaphore_signal(barrier, inc=1, device_id={"mix": flipped(me_m, bit)}, device_id_type=MESH)

    @pl.loop(1, seq)
    def _(i):
        pl.semaphore_signal(barrier, inc=1, device_id={"seq": (me_s + i) % seq}, device_id_type=MESH)

    for copy in local[4:7]:
        copy.wait()
    lane_head = iota((8, width), 1) // HEAD_DIM
    skip_row = jnp.zeros((8, width), F32)
    skips = jnp.broadcast_to(skip[...].astype(F32)[None, :], (8, per))
    for i in range(per):
        skip_row = jnp.where(lane_head == i, skips[:, i : i + 1], skip_row)
    gains = jnp.broadcast_to(gain[...].astype(F32)[None, :], (8, width))
    place = iota((16 - CONV * 2, width), 0)
    par[pl.ds(0, CONV), :] = cx[...]
    par[pl.ds(CONV * 2, 16 - CONV * 2), :] = jnp.where(place == 0, gains, skip_row).astype(BF16)
    par[pl.ds(CONV, CONV), :] = jnp.zeros((CONV, width), BF16)
    pl.semaphore_wait(barrier, len(bits) + seq - 1)

    shards = ((wx, wxb), (par, parb), (wz, wzb), (wo, wob))

    def held(which, offset):
        own, slots = shards[which]
        return own if offset == 0 else slots.at[offset - 1]

    def share(which, offset, bit):
        slot = shards[which][1].at[offset + bit - 1]
        return pltpu.make_async_remote_copy(
            src_ref=held(which, offset), dst_ref=slot,
            send_sem=bsend.at[which, offset + bit - 1], recv_sem=brecv.at[which, offset + bit - 1],
            device_id={"mix": flipped(me_m, bit)}, device_id_type=MESH,
        )

    def low_bit(offset):
        return offset & -offset

    top = bits[-1]
    half, other = me_s % 2, 1 - me_s % 2

    def cross(which):
        own, slots = shards[which]
        return pltpu.make_async_remote_copy(
            src_ref=own.at[half], dst_ref=slots.at[top - 1, half],
            send_sem=xsend.at[which - 2], recv_sem=xrecv.at[which - 2],
            device_id={"mix": flipped(me_m, top)}, device_id_type=MESH,
        )

    def beside(which, part):
        slots = shards[which][1]
        return pltpu.make_async_remote_copy(
            src_ref=slots.at[top - 1, part], dst_ref=slots.at[top - 1, part],
            send_sem=ysend.at[which - 2], recv_sem=yrecv.at[which - 2],
            device_id={"seq": flipped(me_s, 1)}, device_id_type=MESH,
        )

    def is_split(which, offset):
        return which >= 2 and offset == top

    def crossed(which):
        cross(which).wait_recv()
        beside(which, half).start()

    def arrived(which, offset):
        if is_split(which, offset):
            beside(which, other).wait_recv()
        else:
            share(which, offset - low_bit(offset), low_bit(offset)).wait_recv()
        for bit in bits:
            if bit < low_bit(offset):
                share(which, offset, bit).start()

    rim_copy = pltpu.make_async_remote_copy(
        src_ref=tok.at[:, pl.ds(length - RIM, RIM), :], dst_ref=halo,
        send_sem=hsend, recv_sem=hrecv,
        device_id={"seq": (me_s + 1) % seq}, device_id_type=MESH,
    )
    local[0].wait()
    for which in (0, 1):
        for bit in reversed(bits):
            share(which, 0, bit).start()
    local[1].wait()

    @pl.when(me_s < seq - 1)
    def _():
        rim_copy.start()

    @pl.when(me_s == 0)
    def _():
        halo[...] = jnp.zeros_like(halo)

    for which in (2, 3):
        local[which].wait()
        cross(which).start()
        for bit in bits[:-1]:
            share(which, 0, bit).start()

    for copy in local[7:]:
        copy.wait()

    here = iota((LANES, heads), 1)
    there = iota((LANES, heads), 0)
    order = jnp.zeros((LANES, heads), jnp.bool_)
    for offset in range(mix):
        actual = me_m
        for bit in bits:
            if offset & bit:
                actual = flipped(actual, bit)
        order = order | ((there // per == offset) & (here == actual * per + there % per))
    order = order.astype(F32).astype(BF16)
    lower = (iota((BLOCK, BLOCK), 0) >= iota((BLOCK, BLOCK), 1)).astype(F32)
    upper_b = jnp.transpose(lower).astype(BF16)

    totals = []
    for m in range(mixtures):
        device_total = jnp.zeros((1, LANES), F32)
        for b in range(blocks):
            at = pl.ds(b * BLOCK, BLOCK)
            mine = dot(order, rate[m, :, b * BLOCK : (b + 1) * BLOCK])[: heads]
            cum = dot(mine.astype(BF16), upper_b)
            gain_log = jnp.log(jnp.sqrt(one_minus_exp(2.0 * mine)))
            gain_in = jnp.sqrt(one_minus_exp(2.0 * mine))
            tail = jnp.exp(cum[:, BLOCK - 1 :] - cum) * gain_in
            rows_t[m * blocks + b, pl.ds(0, heads), :] = cum - gain_log
            blank = jnp.zeros((LANES - heads, BLOCK), F32)
            cum_t = jnp.transpose(jnp.concatenate([cum, blank], axis=0))
            cums[m, at, :] = cum_t
            ecs[m, at, :] = jnp.exp(cum_t)
            tails[m, at, :] = jnp.transpose(jnp.concatenate([tail, blank], axis=0))
            last = cum_t[BLOCK - 1 :]
            device_total = device_total + last
            totals.append(last)
        logsrc[pl.ds(m, 1), :] = device_total
    logsrc[pl.ds(mixtures, 8 - mixtures), :] = jnp.zeros((8 - mixtures, LANES), F32)
    logs[me_s] = logsrc[...]

    def log_copy(peer):
        return pltpu.make_async_remote_copy(
            src_ref=logsrc, dst_ref=logs.at[me_s], send_sem=lsend, recv_sem=lrecv,
            device_id={"seq": peer}, device_id_type=MESH,
        )

    @pl.loop(1, seq)
    def _(i):
        log_copy((me_s + i) % seq).start()

    def convolve(weight, taps, m, columns):
        total = jnp.zeros((length, columns), F32)
        for k in range(CONV):
            total = total + taps[k : k + 1].astype(F32) * pre[
                m, pl.ds(8 - CONV + 1 + k, length), pl.ds(0, columns)
            ]
        return silu(total)

    def project(weight, m, columns):
        edge = dot(halo[m], weight).astype(BF16).astype(F32)
        pre[m, pl.ds(0, 8), pl.ds(0, columns)] = edge[RIM - 8 :]
        pre[m, pl.ds(8, length), pl.ds(0, columns)] = dot(tok[m], weight).astype(BF16).astype(F32)

    @pl.when(me_s > 0)
    def _():
        rim_copy.wait_recv()

    for m in range(mixtures):
        project(wbc[...], m, 2 * STATE)
        bc = convolve(None, cbc[...], m, 2 * STATE)
        bcs[m] = bc.astype(BF16)
        for b in range(blocks):
            part = bc[b * BLOCK : (b + 1) * BLOCK].astype(BF16)
            bts[m * blocks + b] = jnp.transpose(part.astype(F32))[:STATE].astype(BF16)
            scores = dot_nt(part[:, STATE:], part[:, :STATE])
            cbm[m * blocks + b] = scores * lower

    def flat(weight):
        return weight.reshape(weight.shape[0] * weight.shape[1], weight.shape[2])

    def spread(offset):
        return (iota((LANES, width), 0) == offset * per + iota((LANES, width), 1) // HEAD_DIM).astype(F32).astype(BF16)

    def states(offset):
        weight, params, expand = flat(held(0, offset)[...]), held(1, offset)[...], spread(offset)
        lanes = pl.ds(offset * width, width)
        per_mixture = []
        for m in range(mixtures):
            project(weight, m, width)
            x_act = convolve(None, params, m, width).astype(BF16)
            xact[m, :, lanes] = x_act
            scaled = (x_act.astype(F32) * split_dot(tails[m], expand)).astype(BF16)
            state = None
            for b in range(blocks):
                new = dot(bts[m * blocks + b], scaled[b * BLOCK : (b + 1) * BLOCK])
                if b == 0:
                    state = new
                else:
                    first[m * blocks + b - 1, :, lanes] = state
                    fade = split_dot(jnp.broadcast_to(jnp.exp(totals[m * blocks + b]), (8, LANES)), expand)[:1]
                    state = fade * state + new
            per_mixture.append(state)
        for k in range(seq):
            piece = jnp.concatenate([s[k * nrows : (k + 1) * nrows] for s in per_mixture], axis=0)
            sbuf[offset, k] = piece.astype(BF16)
        rbuf[offset, me_s] = sbuf[offset, me_s]

        @pl.loop(1, seq)
        def _(i):
            state_copy(offset, (me_s + i) % seq).start()

    def state_copy(offset, peer):
        return pltpu.make_async_remote_copy(
            src_ref=sbuf.at[offset, peer], dst_ref=rbuf.at[offset, me_s],
            send_sem=asend.at[offset], recv_sem=arecv.at[offset],
            device_id={"seq": peer}, device_id_type=MESH,
        )

    def carry_copy(offset, peer):
        return pltpu.make_async_remote_copy(
            src_ref=cbuf.at[offset, peer], dst_ref=gbuf.at[offset, me_s],
            send_sem=csend.at[offset], recv_sem=crecv.at[offset],
            device_id={"seq": peer}, device_id_type=MESH,
        )

    def wait_all(ref, sem):
        some = ref.at[pl.ds(0, seq - 1)]
        pltpu.make_async_copy(some, some, sem).wait()

    def carries(offset):
        wait_all(rbuf.at[offset], arecv.at[offset])
        expand = spread(offset)
        fade = split_dot(jnp.exp(logs[...].reshape(seq * 8, LANES)), expand)
        carry = jnp.zeros((mixtures * nrows, width), F32)
        for p in range(seq):
            cbuf[offset, p] = carry.astype(BF16)
            if p < seq - 1:
                down = jnp.concatenate(
                    [jnp.broadcast_to(fade[p * 8 + m : p * 8 + m + 1], (nrows, width)) for m in range(mixtures)], axis=0
                )
                carry = down * carry + rbuf[offset, p].astype(F32)
        gbuf[offset, me_s] = cbuf[offset, me_s]

        @pl.loop(1, seq)
        def _(i):
            carry_copy(offset, (me_s + i) % seq).start()

    group_of = iota((BLOCK, width), 1) // HEAD_DIM

    def intra(offset):
        lanes = pl.ds(offset * width, width)
        skip_row = held(1, offset)[pl.ds(CONV * 2 + 1, 1), :].astype(F32)
        for m in range(mixtures):
            for b in range(blocks):
                at = pl.ds(b * BLOCK, BLOCK)
                scores = cbm[m * blocks + b]
                cum = cums[m, at, :]
                parts = []
                for i in range(per):
                    j = offset * per + i
                    gap = cum[:, j : j + 1] - rows_t[m * blocks + b, pl.ds(j, 1), :]
                    parts.append((jnp.exp(jnp.minimum(gap, 0.0)) * scores).astype(BF16))
                x_act = xact[m, at, lanes]
                full = dot(jnp.concatenate(parts, axis=0), x_act)
                total = full[:BLOCK]
                for i in range(1, per):
                    total = jnp.where(group_of == i, full[i * BLOCK : (i + 1) * BLOCK], total)
                yloc[m, at, lanes] = total + skip_row * x_act.astype(F32)

    def gate(offset):
        lanes = pl.ds(offset * width, width)
        weight = flat(held(2, offset)[...])
        for m in range(mixtures):
            sgate[m, :, lanes] = silu(dot(tok[m], weight).astype(BF16).astype(F32))

    same_head = (iota((width, width), 0) // HEAD_DIM == iota((width, width), 1) // HEAD_DIM).astype(F32).astype(BF16)

    def finish(offset):
        lanes = pl.ds(offset * width, width)
        wait_all(gbuf.at[offset], crecv.at[offset])
        expand = spread(offset)
        gain_row = held(1, offset)[pl.ds(CONV * 2, 1), :].astype(F32)
        for m in range(mixtures):
            state = jnp.concatenate(
                [gbuf[offset, k].astype(F32)[m * nrows : (m + 1) * nrows] for k in range(seq)], axis=0
            )
            grow = split_dot(ecs[m], expand)
            for b in range(blocks):
                at = pl.ds(b * BLOCK, BLOCK)
                if b > 0:
                    fade = split_dot(jnp.broadcast_to(jnp.exp(totals_sum(m, b)), (8, LANES)), expand)[:1]
                    incoming = fade * state + first[m * blocks + b - 1, :, lanes]
                else:
                    incoming = state
                inter = dot(bcs[m, at, :][:, STATE:], incoming.astype(BF16))
                y = yloc[m, at, lanes] + grow[b * BLOCK : (b + 1) * BLOCK] * inter
                v = y * sgate[m, at, lanes]
                power = split_dot(v * v, same_head) * (1.0 / HEAD_DIM)
                normed[m, at, lanes] = (v * lax.rsqrt(power + 1e-05) * gain_row).astype(BF16)

    def totals_sum(m, b):
        total = totals[m * blocks]
        for k in range(1, b):
            total = total + totals[m * blocks + k]
        return total

    def take(which, offset):
        if offset:
            arrived(which, offset)

    def logs_arrived():
        some = logs.at[pl.ds(0, seq - 1)]
        pltpu.make_async_copy(some, some, lrecv).wait()

    for offset in range(top):
        take(1, offset)
        take(0, offset)
        states(offset)
        intra(offset)
    for offset in range(top):
        take(2, offset)
        gate(offset)
    for offset in range(top, mix):
        take(1, offset)
        take(0, offset)
        states(offset)
    logs_arrived()
    for offset in range(top):
        carries(offset)
        take(3, offset)
    crossed(2)
    for offset in range(top, mix):
        intra(offset)
        if offset == top:
            carries(offset)
            crossed(3)
    take(2, top)
    for offset in range(top + 1, mix):
        carries(offset)
    finish(0)
    gate(top)
    take(3, top)
    for offset in range(1, top):
        finish(offset)
    for offset in range(top + 1, mix):
        take(2, offset)
        gate(offset)
    for offset in range(top, mix):
        finish(offset)
        if offset > top:
            take(3, offset)
    for m in range(mixtures):
        total = jnp.zeros((length, wo.shape[2]), F32)
        for offset in range(mix):
            total = total + dot(normed[m, :, pl.ds(offset * width, width)], flat(held(3, offset)[...]))
        out[m] = total.astype(BF16)

    @pl.when(me_s < seq - 1)
    def _():
        rim_copy.wait_send()

    for which in range(4):
        for offset in range(mix):
            for bit in bits:
                if (offset == 0 or bit < low_bit(offset)) and not is_split(which, offset + bit):
                    share(which, offset, bit).wait_send()
    for which in (2, 3):
        cross(which).wait_send()
        beside(which, half).wait_send()
    wait_all(logs, lsend)
    for offset in range(mix):
        wait_all(sbuf.at[offset], asend.at[offset])
        wait_all(cbuf.at[offset], csend.at[offset])


def solution(mesh):
    seq, mix = mesh.shape["seq"], mesh.shape["mix"]

    def body(tokens, log_forget_rate, w_x, w_z, w_bc, conv_x, conv_bc, skip, gain, w_out):
        mixtures, length, depth = tokens.shape
        width = w_x.shape[1]
        rate = jnp.transpose(log_forget_rate, (0, 2, 1))
        inner = width * mix
        blocks = length // BLOCK
        w_x, w_z, w_out = (w.reshape(2, w.shape[0] // 2, w.shape[1]) for w in (w_x, w_z, w_out))
        vmem = pl.BlockSpec(memory_space=pltpu.VMEM)
        hbm = pl.BlockSpec(memory_space=pltpu.HBM)
        dma = pltpu.SemaphoreType.DMA
        rows = mixtures * (STATE // seq)
        return pl.pallas_call(
            functools.partial(kernel, seq, mix),
            out_shape=jax.ShapeDtypeStruct((mixtures, length, w_out.shape[2]), BF16),
            in_specs=[hbm] * 10,
            out_specs=vmem,
            scratch_shapes=[
                *[
                    pltpu.VMEM(a.shape, BF16)
                    for a in (tokens, rate, w_x, w_z, w_bc, conv_x, conv_bc, skip, gain, w_out)
                ],
                pltpu.VMEM((16, width), BF16),
                pltpu.VMEM((mixtures, RIM, depth), BF16),
                pltpu.VMEM((mix - 1,) + w_x.shape, BF16),
                pltpu.VMEM((mix - 1,) + w_z.shape, BF16),
                pltpu.VMEM((mix - 1,) + w_out.shape, BF16),
                pltpu.VMEM((mix - 1, 16, width), BF16),
                pltpu.VMEM((seq, 8, LANES), F32),
                pltpu.VMEM((8, LANES), F32),
                pltpu.VMEM((mixtures, 8 + length, width), F32),
                pltpu.VMEM((mixtures, length, inner), BF16),
                pltpu.VMEM((mixtures, length, 2 * STATE), BF16),
                pltpu.VMEM((mixtures * blocks, STATE, BLOCK), BF16),
                pltpu.VMEM((mixtures, length, LANES), F32),
                pltpu.VMEM((mixtures, length, LANES), F32),
                pltpu.VMEM((mixtures, length, LANES), F32),
                pltpu.VMEM((mixtures * blocks, LANES, BLOCK), F32),
                pltpu.VMEM((mixtures * blocks, BLOCK, BLOCK), F32),
                pltpu.VMEM((mixtures * blocks, STATE, inner), F32),
                pltpu.VMEM((mixtures, length, inner), F32),
                pltpu.VMEM((mixtures, length, inner), F32),
                pltpu.VMEM((mixtures, length, inner), BF16),
                pltpu.VMEM((mix, seq, rows, width), BF16),
                pltpu.VMEM((mix, seq, rows, width), BF16),
                pltpu.VMEM((mix, seq, rows, width), BF16),
                pltpu.VMEM((mix, seq, rows, width), BF16),
                dma((10,)),
                dma((4, mix - 1)),
                dma((4, mix - 1)),
                dma((2,)),
                dma((2,)),
                dma((2,)),
                dma((2,)),
                dma,
                dma,
                dma,
                dma,
                dma,
                dma((mix,)),
                dma((mix,)),
                dma((mix,)),
                dma((mix,)),
            ],
            compiler_params=pltpu.CompilerParams(
                collective_id=0, has_side_effects=True, vmem_limit_bytes=54 * 1024 * 1024
            ),
        )(tokens, rate, w_x, w_z, w_bc, conv_x, conv_bc, skip, gain, w_out)

    return jax.shard_map(
        body,
        mesh=mesh,
        in_specs=(
            P("mix", "seq", None),
            P("mix", "seq", None),
            P(None, "mix"),
            P(None, "mix"),
            P(),
            P(None, "mix"),
            P(),
            P("mix"),
            P("mix"),
            P("mix", None),
        ),
        out_specs=P("mix", "seq", None),
        check_vma=False,
    )
```
